256 devices in a mesh: grp: 8 (over x, y_hi), feat: 32 (over y_lo, z, core).
Axes of the slice: x: 4, y: 4 (y_hi: 2, y_lo: 2; y = y_hi * 2 + y_lo), z: 8, core: 2. Of those that a mesh axis runs over, the one named last changes fastest.
Arguments:
- resid: bfloat16 [4, 512, 2304], P(None, 'grp'), may hold values from -6 to 6
- w_enc: bfloat16 [4, 2304, 8192], P(None, None, 'feat'), may hold values from -0.125 to 0.125
- b_enc: float32 [4, 8192], P(None, 'feat'), may hold values from -3 to 3
- w_dec: bfloat16 [4, 8, 8192, 2304], P(None, 'grp', 'feat'), may hold values from -0.0625 to 0.0625
- targets: bfloat16 [8, 512, 2304], P('grp'), may hold values from -6 to 6
- start_layer: int32 [4, 32], P(None, 'feat'), may hold values from 0 to 7, as said below
Outputs:
- active: bfloat16 [512, 4, 8192], P('grp', None, 'feat')
- recon: bfloat16 [8, 512, 2304], P('grp', 'feat')
- recon_loss: float32 [], replicated
- feat_grad: float32 [512, 4, 8192], P('grp', None, 'feat')
The draws below stay inside these ranges and needn't reach their ends.
Inputs may be any that keep to these rules, and one draw needn't show every extreme that they name: `start_layer`: each column is nondecreasing over source layers; in every column the first source feeds from target 0 and the last source feeds only target 8 - 1.
All inputs are finite; a program needn't handle non-finite values.
Results may differ from the reference program's by a relative error of at most 0.0049.
Values may be sent and summed in bfloat16 or wider, within the bound.
A program may use at most 64 MiB of HBM per device.

```python
import jax
import jax.numpy as jnp
from jax import lax

D = 2304
F = 8192
L_SRC = 4
TOK = 512
L_TGT = 8
N_FEAT = 32


def draw_start_layer(key, part):
    middle = jnp.sort(jax.random.randint(key, (L_SRC - 2, N_FEAT), 0, L_TGT), axis=0).astype(jnp.int32)
    first_row = jnp.zeros((1, N_FEAT), jnp.int32)
    last_row = jnp.full((1, N_FEAT), L_TGT - 1, jnp.int32)
    return jnp.concatenate([first_row, middle, last_row], axis=0)


def levels(rng, dims, shards, smallest, largest):
    level = 1.0
    for dim, parts in shards:
        steps = jax.random.uniform(jax.random.fold_in(jax.random.fold_in(rng, 6), dim), (parts,), jnp.float32, smallest / len(shards), largest / len(shards))
        level = level * jnp.repeat(jnp.exp(steps), dims[dim] // parts).reshape((-1,) + (1,) * (len(dims) - 1 - dim))
    return level


def bell_draw(key, extent, width, bound, shards=(), kind=jnp.bfloat16):
    result = jax.random.normal(key, extent, jnp.float32) * width
    if len(shards) > 0:
        result = levels(key, extent, shards, -0.22, 0.18) * result
    return jnp.clip(result, min=-bound, max=bound).astype(kind)


def setup_inputs(seed: int = 0) -> dict:
    keys = jax.random.split(jax.random.key(seed), 7)
    return {
        "resid": bell_draw(keys[0], (L_SRC, TOK, D), 1.0, 6.0, ((1, 8),)),
        "w_enc": bell_draw(keys[1], (L_SRC, D, F), D ** -0.5, 0.125, ((2, 32),)),
        "b_enc": bell_draw(keys[2], (L_SRC, F), 0.5, 3.0, ((1, 32),), jnp.float32),
        "w_dec": bell_draw(keys[3], (L_SRC, L_TGT, F, D), F ** -0.5, 0.0625, ((1, 8), (2, 32))),
        "targets": bell_draw(keys[4], (L_TGT, TOK, D), 1.0, 6.0, ((0, 8),)),
        "start_layer": draw_start_layer(jax.random.fold_in(keys[6], 71), 0),
    }


def feeding(start_layer):
    target_ids = jnp.arange(L_TGT, dtype=jnp.int32)
    return (target_ids[None, :, None] >= start_layer[:, None, :]).astype(jnp.float32)


def reference(resid, w_enc, b_enc, w_dec, targets, start_layer):
    feeds_mask = feeding(start_layer)
    encoded = []
    for source in range(L_SRC):
        pre_act = jnp.dot(resid[source], w_enc[source], preferred_element_type=jnp.float32) + b_enc[source]
        encoded.append(jnp.maximum(pre_act, 0.0).astype(jnp.bfloat16))
    active = jnp.stack(encoded, axis=1)
    block_width = F // N_FEAT
    recon_list = []
    for target in range(L_TGT):
        def add_block(index, summed):
            first_col = (index * block_width).astype(jnp.int32)
            columns = lax.dynamic_slice_in_dim(active, first_col, block_width, 2)
            weights = lax.dynamic_slice_in_dim(w_dec[:, target], first_col, block_width, 1)
            block_mask = lax.dynamic_index_in_dim(feeds_mask[:, target, :], index, 1, False)
            term = jnp.zeros((TOK, D), jnp.float32)
            for source in range(L_SRC):
                term = term + block_mask[source] * jnp.dot(columns[:, source], weights[source], preferred_element_type=jnp.float32)
            return summed + term
        recon_list.append(lax.fori_loop(0, N_FEAT, add_block, jnp.zeros((TOK, D), jnp.float32)))
    recon_full = jnp.stack(recon_list, axis=0)
    difference = recon_full - targets.astype(jnp.float32)
    error_rows = difference.astype(jnp.bfloat16)
    recon_loss = jnp.sum(difference * difference) / (L_TGT * TOK * D)
    gradients = []
    for source in range(L_SRC):
        summed = jnp.zeros((TOK, F), jnp.float32)
        for target in range(L_TGT):
            column_mask = jnp.repeat(feeds_mask[source, target], block_width)
            summed = summed + column_mask[None, :] * lax.dot_general(error_rows[target], w_dec[source, target], (((1,), (1,)), ((), ())), preferred_element_type=jnp.float32)
        gradients.append(summed)
    feat_grad = jnp.stack(gradients, axis=1)
    return active, recon_full.astype(jnp.bfloat16), recon_loss, feat_grad
```

```python
import jax
import jax.numpy as jnp
from jax import lax
from jax.experimental import pallas as pl
from jax.experimental.pallas import tpu as pltpu
from jax.sharding import PartitionSpec as P

MESH = pl.DeviceIdType.MESH
BF = jnp.bfloat16
F32 = jnp.float32

NX, NZ = 4, 8
GRP, FEAT = 8, 32
SRC, TOKENS, WIDTH, BLOCK = 4, 512, 2304, 256
OWN = TOKENS // GRP
ROWS = TOKENS // FEAT
ALL_K = SRC * BLOCK
CUT = 1024
CA, CB = slice(0, CUT), slice(CUT, WIDTH)
WA, WB = CUT, WIDTH - CUT
TILE = 256
N_SEMS = 256


class Net:
    def __init__(self, send_sems, recv_sems):
        self.send_sems, self.recv_sems = send_sems, recv_sems
        self.copies = {}

    def send(self, key, src, dst, device):
        n = len(self.copies)
        copy = pltpu.make_async_remote_copy(
            src_ref=src,
            dst_ref=dst,
            send_sem=self.send_sems.at[n],
            recv_sem=self.recv_sems.at[n],
            device_id=device,
            device_id_type=MESH,
        )
        self.copies[key] = copy
        copy.start()

    def arrived(self, key):
        self.copies[key].wait_recv()

    def finish(self):
        for copy in self.copies.values():
            copy.wait_send()


def kernel(
    resid, w_enc, b_enc, w_dec, targets, start,
    act_out, recon_out, loss_out, grad_out,
    resid_v, wenc_v, wdec_v, targ_v, act_all, lhs, part, x_out, x_in, y_out, y_in,
    za_out, za_in, zb_out, zb_in, ya_out, ya_in, own, err, grads,
    r_out, r_in, q_out, q_in, ry_out, ry_in, lz, lc, lg, vsum,
    load_sems, send_sems, recv_sems,
):
    g, f = lax.axis_index("grp"), lax.axis_index("feat")
    x, yh = lax.div(g, 2), lax.rem(g, 2)
    c = lax.rem(f, 2)
    z = lax.rem(lax.div(f, 2), NZ)
    yl = lax.div(f, 2 * NZ)

    def feat_of(yl_, z_, c_):
        return (yl_ * NZ + z_) * 2 + c_

    def zat(d):
        return lax.rem(z + d + NZ, NZ)

    def xat(d):
        return lax.rem(x + d + NX, NX)

    partner = (g, feat_of(yl, z, 1 - c))
    yside = (g, feat_of(1 - yl, z, c))
    zside = {d: (g, feat_of(yl, zat(d), c)) for d in (1, -1)}
    gpair = (x * 2 + 1 - yh, f)
    xside = {d: (xat(d) * 2 + yh, f) for d in (1, -1)}
    spot = yl * 2 + c

    def flip(a, m, bits):
        out = 0
        for b in range(bits):
            bit = lax.rem(lax.div(a, 1 << b), 2)
            out = out + ((1 - bit) if (m >> b) & 1 else bit) * (1 << b)
        return out

    zpeers = {d: (g, feat_of(yl, zat(d), c)) for d in range(1, NZ)}

    def spot_peer(m):
        s = flip(spot, m, 2)
        return (g, feat_of(lax.div(s, 2), z, lax.rem(s, 2)))

    spots = {m: spot_peer(m) for m in range(1, 4)}
    gpeers = {m: (flip(g, m, 3), f) for m in range(1, GRP)}

    barrier = pltpu.get_barrier_semaphore()
    peers = [*zpeers.values(), *spots.values(), *gpeers.values()]
    for peer in peers:
        pl.semaphore_signal(barrier, inc=1, device_id=peer, device_id_type=MESH)

    loads = []

    def load(src, dst):
        copy = pltpu.make_async_copy(src, dst, load_sems.at[len(loads)])
        loads.append(copy)
        copy.start()
        return copy

    enc_loads = [(load(resid.at[s], resid_v.at[s]), load(w_enc.at[s], wenc_v.at[s])) for s in range(SRC)]
    dec_loads = [load(w_dec.at[s, 0], wdec_v.at[pl.ds(s * BLOCK, BLOCK)]) for s in range(SRC)]
    targ_load = load(targets.at[0, pl.ds(f * ROWS, ROWS)], targ_v)

    net = Net(send_sems, recv_sems)
    feeds = [jnp.where(g >= start[s, 0], 1.0, 0.0).astype(F32) for s in range(SRC)]

    def act_at(group, s, half=None):
        first = group * 2 if half is None else group * 2 + half
        return act_all.at[pl.ds(first, 2 if half is None else 1), :, :, pl.ds(s * BLOCK, BLOCK)]

    for s in range(SRC):
        for copy in enc_loads[s]:
            copy.wait()
        pre = jnp.dot(resid_v[s], wenc_v[s], preferred_element_type=F32) + b_enc[pl.ds(s, 1), :]
        a = jnp.maximum(pre, 0.0).astype(BF)
        act_out[s] = a
        act_all[pl.ds(g * 2, 2), :, :, pl.ds(s * BLOCK, BLOCK)] = a.reshape(2, 2, ROWS, BLOCK)
        if s == 0:
            pl.semaphore_wait(barrier, len(peers))
        mine = act_at(g, s)
        net.send(("a", s), mine, mine, gpair)
        for d in (1, -1):
            net.send(("x", s, d), mine, mine, xside[d])
    other = x * 2 + 1 - yh
    for s in range(SRC):
        net.arrived(("a", s))
        block = act_at(other, s)
        for d in (1, -1):
            net.send(("xy", s, d), block, block, xside[d])
    for kind, row in (("x", yh), ("xy", 1 - yh)):
        for s in range(SRC):
            for half, d in ((0, 1), (1, -1)):
                net.arrived((kind, s, d))
                block = act_at(xat(-d) * 2 + row, s, half)
                net.send((kind + "f", s, d), block, block, xside[d])
    for kind in ("xf", "xyf"):
        for s in range(SRC):
            for d in (1, -1):
                net.arrived((kind, s, d))

    for copy in dec_loads:
        copy.wait()
    feed_row = jnp.concatenate([jnp.full((1, BLOCK), feeds[s], F32) for s in range(SRC)], axis=1)

    @pl.loop(0, 2 * NZ)
    def _(i):
        for h in range(2):
            lhs[h, i] = (act_all[i, h].astype(F32) * feed_row).astype(BF)

    def decode(core, first, tiles, out):
        @pl.loop(0, tiles)
        def _(n):
            cols = pl.ds(pl.multiple_of(first + n * TILE, TILE), TILE)
            a = lhs[core].reshape(2 * NZ * ROWS, ALL_K)
            p = jnp.dot(a, wdec_v[:, cols], preferred_element_type=F32)
            out[:, :, cols] = p.reshape(2 * NZ, ROWS, TILE).astype(out.dtype)

    decode(1 - c, CUT, WB // TILE, x_out)
    net.send("pB", x_out.at[:, :, CB], x_in.at[:, :, CB], partner)
    decode(1 - c, 0, WA // TILE, x_out)
    net.send("pA", x_out.at[:, :, CA], x_in.at[:, :, CA], partner)
    decode(c, CUT, WB // TILE, part)

    def chip(row, cols):
        return part[row, :, cols] + x_in[row, :, cols].astype(F32)

    z_order = (4, -3, 3, -2, 2, -1, 1, 0)
    net.arrived("pB")
    for i, d in enumerate(z_order):
        y_out[i] = chip((1 - yl) * NZ + zat(d), CB).astype(BF)
        net.send(("y", d), y_out.at[i], y_in.at[i], yside)
    decode(c, 0, WA // TILE, part)
    net.arrived("pA")

    first_way = {0: -1, 1: 1, 2: -1}

    def own_sum(stream, d):
        if stream == 0:
            return chip((1 - yl) * NZ + zat(d), CA)
        if stream == 1:
            return chip(yl * NZ + zat(d), CA)
        i = z_order.index(d if d > -4 else 4)
        net.arrived(("y", z_order[i]))
        return chip(yl * NZ + zat(d), CB) + y_in[i].astype(F32)

    def ring_in(stream, way, k):
        net.arrived(("z", stream, way, k))
        i = 0 if way < 0 else 1
        return (zb_in[i, k] if stream == 2 else za_in[stream, i, k]).astype(F32)

    def hop(stream, k):
        for way in (-1, 1):
            if k == 0 and way != first_way[stream]:
                continue
            value = own_sum(stream, way * (4 - k))
            if k > 1 or (k == 1 and way == first_way[stream]):
                value = value + ring_in(stream, way, k - 1)
            i = 0 if way < 0 else 1
            out, into = (zb_out, zb_in) if stream == 2 else (za_out.at[stream], za_in.at[stream])
            out[i, k] = value.astype(BF)
            net.send(("z", stream, way, k), out.at[i, k], into.at[i, k], zside[way])

    def last(stream):
        return own_sum(stream, 0) + ring_in(stream, -1, 3) + ring_in(stream, 1, 3)

    targ_load.wait()
    hop(0, 0)
    hop(1, 0)
    hop(2, 0)
    for k in (1, 2, 3):
        for stream in (0, 1, 2):
            hop(stream, k)
    ya_out[...] = last(0).astype(BF)
    net.send("ya", ya_out, ya_in, yside)
    own[...] = last(1)

    def close(value, cols):
        recon_out[:, cols] = value.astype(BF)
        diff = value - targ_v[:, cols].astype(F32)
        err[c, yl, z, :, cols] = diff.astype(BF)
        square = diff * diff
        total = square[:, 0:128]
        for i in range(1, square.shape[1] // 128):
            total = total + square[:, i * 128 : (i + 1) * 128]
        return total[0:8] + total[8:16]

    def err_at(y, d, cols=None):
        z_ = zat(d)
        return err.at[c, y, z_] if cols is None else err.at[c, y, z_, :, cols]

    loss = close(last(2), CB)
    far = {0: -1, 1: 1, 2: -1}

    def spread(stream, way, k):
        y, cols = ((yl, CA), (1 - yl, CA), (yl, CB))[stream]
        if k < 3 or (k == 3 and way == far[stream]):
            block = err_at(y, -way * k, cols)
            net.send(("e", stream, way, k + 1), block, block, zside[way])

    for way in (-1, 1):
        spread(2, way, 0)
    block = err_at(yl, 0, CB)
    net.send(("eyB", 0, 0), block, block, yside)
    net.arrived("ya")
    loss = loss + close(own[...] + ya_in[...].astype(F32), CA)
    block = err_at(yl, 0, CA)
    net.send("eyA", block, block, yside)
    for way in (-1, 1):
        spread(0, way, 0)
    block = err_at(yl, 0)
    net.send(("p0", 0, 0), block, block, partner)

    lz[z] = loss
    for d in range(1, NZ):
        net.send(("lz", d), lz.at[z], lz.at[z], zpeers[d])

    net.arrived("eyA")
    for way in (-1, 1):
        spread(1, way, 0)

    def total_of(slots, n):
        total = slots[0]
        for i in range(1, n):
            total = total + slots[i]
        return total

    def to_partner_y(way, k):
        net.arrived(("eyB", way, k))
        block = err_at(1 - yl, -way * k)
        net.send(("p1", way, k), block, block, partner)

    def gradient(steps):
        ds = [-way * k if way else k for way, k in steps]
        for way, k in steps:
            net.arrived(("p0", way, k))
            net.arrived(("p1", way, k))
        rows = jnp.concatenate([err[:, :, zat(d)].reshape(4 * ROWS, WIDTH) for d in ds], axis=0)
        for s in range(SRC):
            p = lax.dot_general(
                rows, wdec_v[pl.ds(s * BLOCK, BLOCK), :], (((1,), (1,)), ((), ())), preferred_element_type=F32
            )
            p = p * feeds[s]
            for j, d in enumerate(ds):
                for core in range(2):
                    for y in range(2):
                        r = (j * 4 + core * 2 + y) * ROWS
                        grads[y * NZ + zat(d), core, :, pl.ds(s * BLOCK, BLOCK)] = p[r : r + ROWS]

    steps_of = {k: [(-1, k), (1, k)] for k in (1, 2, 3)}
    steps_of[0] = [(0, 0)]
    steps_of[4] = [(0, 4)]

    to_partner_y(0, 0)
    for k in (1, 2, 3):
        for way in (-1, 1):
            net.arrived(("e", 2, way, k))
            spread(2, way, k)
            block = err_at(yl, -way * k, CB)
            net.send(("eyB", way, k), block, block, yside)
        for way in (-1, 1):
            net.arrived(("e", 0, way, k))
            spread(0, way, k)
            block = err_at(yl, -way * k)
            net.send(("p0", way, k), block, block, partner)
        for way in (-1, 1):
            net.arrived(("e", 1, way, k))
            spread(1, way, k)
        gradient(steps_of[k - 1])
        if k == 1:
            for d in range(1, NZ):
                net.arrived(("lz", d))
            lc[spot] = total_of(lz, NZ)
            for m in spots:
                net.send(("lc", m), lc.at[spot], lc.at[spot], spots[m])
        if k == 2:
            for m in spots:
                net.arrived(("lc", m))
            lg[g] = total_of(lc, 4)
            for m in gpeers:
                net.send(("lg", m), lg.at[g], lg.at[g], gpeers[m])
        for way in (-1, 1):
            to_partner_y(way, k)
    net.arrived(("e", 2, far[2], 4))
    block = err_at(yl, 4, CB)
    net.send(("eyB", 0, 4), block, block, yside)
    net.arrived(("e", 0, far[0], 4))
    block = err_at(yl, 4)
    net.send(("p0", 0, 4), block, block, partner)
    net.arrived(("e", 1, far[1], 4))
    gradient(steps_of[3])
    net.arrived(("eyB", 0, 4))
    block = err_at(1 - yl, 4)
    net.send(("p1", 0, 4), block, block, partner)
    for m in gpeers:
        net.arrived(("lg", m))
    loss_out[0, 0] = jnp.sum(total_of(lg, GRP)) / (GRP * TOKENS * WIDTH)
    gradient(steps_of[4])

    def grad_at(xd, pair, s):
        row = 1 - yh if pair else yh
        return grads[pl.ds((xat(xd) * 2 + row) * 2, 2), :, :, pl.ds(s * BLOCK, BLOCK)].reshape(OWN, BLOCK)

    ways = {-1: True, 1: False}
    for s in range(SRC):
        for way in (-1, 1):
            i = 0 if way < 0 else 1
            r_out[s, i, 0] = grad_at(2, ways[way], s).astype(BF)
            net.send(("r", s, way, 0), r_out.at[s, i, 0], r_in.at[s, i, 0], xside[way])
        for way in (-1, 1):
            i = 0 if way < 0 else 1
            q_out[s, i] = grad_at(way, not ways[way], s).astype(BF)
            net.send(("q", s, way), q_out.at[s, i], q_in.at[s, i], xside[way])
    for s in range(SRC):
        for way in (-1, 1):
            i = 0 if way < 0 else 1
            net.arrived(("r", s, way, 0))
            r_out[s, i, 1] = (grad_at(way, ways[way], s) + r_in[s, i, 0].astype(F32)).astype(BF)
            net.send(("r", s, way, 1), r_out.at[s, i, 1], r_in.at[s, i, 1], xside[way])
    for s in range(SRC):
        net.arrived(("q", s, 1))
        net.arrived(("q", s, -1))
        net.arrived(("r", s, -1, 1))
        u = grad_at(0, True, s) + r_in[s, 0, 1].astype(F32) + q_in[s, 1].astype(F32)
        ry_out[s] = u.astype(BF)
        net.send(("ry", s), ry_out.at[s], ry_in.at[s], gpair)
        net.arrived(("r", s, 1, 1))
        vsum[s] = grad_at(0, False, s) + r_in[s, 1, 1].astype(F32) + q_in[s, 0].astype(F32)
    for s in range(SRC):
        net.arrived(("ry", s))
        grad_out[s] = vsum[s] + ry_in[s].astype(F32)
    net.finish()


def per_device(resid, w_enc, b_enc, w_dec, targets, start_layer):
    vmem = pl.BlockSpec(memory_space=pltpu.VMEM)
    smem = pl.BlockSpec(memory_space=pltpu.SMEM)
    anywhere = pl.BlockSpec(memory_space=pl.ANY)
    blocks = 2 * NZ
    act, recon, loss, grad = pl.pallas_call(
        kernel,
        out_shape=(
            jax.ShapeDtypeStruct((SRC, OWN, BLOCK), BF),
            jax.ShapeDtypeStruct((ROWS, WIDTH), BF),
            jax.ShapeDtypeStruct((1, 1), F32),
            jax.ShapeDtypeStruct((SRC, OWN, BLOCK), F32),
        ),
        in_specs=[anywhere, anywhere, vmem, anywhere, anywhere, smem],
        out_specs=(vmem, vmem, smem, vmem),
        scratch_shapes=[
            pltpu.VMEM((SRC, OWN, WIDTH), BF),
            pltpu.VMEM((SRC, WIDTH, BLOCK), BF),
            pltpu.VMEM((ALL_K, WIDTH), BF),
            pltpu.VMEM((ROWS, WIDTH), BF),
            pltpu.VMEM((blocks, 2, ROWS, ALL_K), BF),
            pltpu.VMEM((2, blocks, ROWS, ALL_K), BF),
            pltpu.VMEM((blocks, ROWS, WIDTH), F32),
            pltpu.VMEM((blocks, ROWS, WIDTH), BF),
            pltpu.VMEM((blocks, ROWS, WIDTH), BF),
            pltpu.VMEM((NZ, ROWS, WB), BF),
            pltpu.VMEM((NZ, ROWS, WB), BF),
            pltpu.VMEM((2, 2, 4, ROWS, WA), BF),
            pltpu.VMEM((2, 2, 4, ROWS, WA), BF),
            pltpu.VMEM((2, 4, ROWS, WB), BF),
            pltpu.VMEM((2, 4, ROWS, WB), BF),
            pltpu.VMEM((ROWS, WA), BF),
            pltpu.VMEM((ROWS, WA), BF),
            pltpu.VMEM((ROWS, WA), F32),
            pltpu.VMEM((2, 2, NZ, ROWS, WIDTH), BF),
            pltpu.VMEM((blocks, 2, ROWS, ALL_K), F32),
            pltpu.VMEM((SRC, 2, 2, OWN, BLOCK), BF),
            pltpu.VMEM((SRC, 2, 2, OWN, BLOCK), BF),
            pltpu.VMEM((SRC, 2, OWN, BLOCK), BF),
            pltpu.VMEM((SRC, 2, OWN, BLOCK), BF),
            pltpu.VMEM((SRC, OWN, BLOCK), BF),
            pltpu.VMEM((SRC, OWN, BLOCK), BF),
            pltpu.VMEM((NZ, 8, 128), F32),
            pltpu.VMEM((4, 8, 128), F32),
            pltpu.VMEM((GRP, 8, 128), F32),
            pltpu.VMEM((SRC, OWN, BLOCK), F32),
            pltpu.SemaphoreType.DMA((16,)),
            pltpu.SemaphoreType.DMA((N_SEMS,)),
            pltpu.SemaphoreType.DMA((N_SEMS,)),
        ],
        compiler_params=pltpu.CompilerParams(
            collective_id=0, has_side_effects=True, vmem_limit_bytes=60 * 1024 * 1024
        ),
    )(resid, w_enc, b_enc, w_dec, targets, start_layer)
    return (
        act.transpose(1, 0, 2),
        recon[None],
        loss[0, 0],
        grad.transpose(1, 0, 2),
    )


def solution(mesh):
    in_specs = (
        P(None, "grp", None),
        P(None, None, "feat"),
        P(None, "feat"),
        P(None, "grp", "feat", None),
        P("grp", None, None),
        P(None, "feat"),
    )
    out_specs = (P("grp", None, "feat"), P("grp", "feat", None), P(), P("grp", None, "feat"))
    return jax.shard_map(
        per_device, mesh=mesh, in_specs=in_specs, out_specs=out_specs, check_vma=False
    )
```
